32 devices in a mesh: atm: 8 (over z, x), cpl: 4 (over y, core).
Axes of the slice: x: 2, y: 2, z: 4, core: 2. Of those that a mesh axis runs over, the one named last changes fastest.
Arguments:
- state: bfloat16 [16384, 32, 128], P(('atm', 'cpl')), may hold values from -6 to 6
- cosine_zenith: bfloat16 [16384], P(('atm', 'cpl')), may hold values from 0.25 to 1
- sunlit: int32 [16384], P(('atm', 'cpl')), may hold values from 0 to 1, as said below
- kcoef: bfloat16 [32, 256], replicated, may hold values from -1 to 1
- scatter_coef: bfloat16 [32, 256], replicated, may hold values from -1 to 1
- gpoint_weight: float32 [256], replicated, may hold values from 0.3 to 3
- sea_temp: float32 [16384], P(('atm', 'cpl')), may hold values from -6 to 6
- intersection_col: int32 [16384, 4], P(('atm', 'cpl')), may hold values from 0 to 2047
- intersection_weight: int32 [16384, 4], P(('atm', 'cpl')), may hold values from 1 to 8
- nearest_ocean: int32 [16384], P(('atm', 'cpl')), may hold values from 0 to 2047
Outputs:
- heating_rate: float32 [16384, 128], P(('atm', 'cpl'))
- sea_temp_next: float32 [16384], P(('atm', 'cpl'))
- column_sea_temp: float32 [16384], P(('atm', 'cpl'))
The draws below stay inside these ranges and needn't reach their ends.
Inputs may be any that keep to these rules, and one draw needn't show every extreme that they name: On each device the number of sunlit columns is a multiple of 8; the two devices of one cpl index whose atm indices differ by 4 together hold exactly 512 sunlit columns. `intersection_col`: Indexes, in cpl order, the columns held by the 4 devices that share the ocean cell's atm index. `nearest_ocean`: Indexes, in cpl order, the ocean cells held by the 4 devices that share the column's atm index.
All inputs are finite; a program needn't handle non-finite values.
Results may differ from the reference program's by a relative error of at most 0.0006.
Values may be sent and summed in bfloat16 or wider, within the bound.
A program may use at most 64 MiB of HBM per device.

```python
import math
import jax
import jax.numpy as jnp
from jax import lax

LEV = 128
G = 256
FEAT = 32
NOV = 4
COL_DEV = 512
OCN_DEV = 512
COLS = 16384
OCELLS = 16384
N_ATM = 8
N_CPL = 4


def draw_sunlit(key, part):
    per_peer = COL_DEV // N_ATM
    half = N_ATM // 2
    key_rot, key_split, key_cols = jax.random.split(key, 3)
    rotation = jax.random.randint(key_rot, (N_CPL,), 0, N_ATM)
    partial_sun = jax.random.randint(key_split, (N_CPL,), 0, per_peer + 1)
    atm_index = jnp.arange(N_ATM, dtype=jnp.int32)[:, None]
    offset = (atm_index - rotation[None, :]) % N_ATM
    blocks = jnp.where(offset < half - 1, per_peer, 0)
    blocks = jnp.where(offset == half - 1, per_peer - partial_sun[None, :], blocks)
    blocks = jnp.where(offset == N_ATM - 1, partial_sun[None, :], blocks)
    counts = (blocks * N_ATM).reshape(-1)
    device_keys = jax.random.split(key_cols, N_ATM * N_CPL)
    ranks = jax.vmap(lambda single: jax.random.permutation(single, COL_DEV))(device_keys)
    return (ranks < counts[:, None]).astype(jnp.int32).reshape(-1)


def place_ends(entries, own_key, least, high):
    longest = entries.shape.index(max(entries.shape))
    spots = []
    for shift in (0, 1):
        where = [jax.random.randint(jax.random.fold_in(own_key, axis), (), 0, length) for axis, length in enumerate(entries.shape)]
        where[longest] = (where[longest] + shift) % entries.shape[longest]
        spots.append(tuple(where))
    return entries.at[spots[0]].set(least).at[spots[1]].set(high)


def shard_levels(own_key, extent, pieces, low, top_value):
    gain, own = 1.0, jax.random.fold_in(own_key, 6)
    for axis_at, blocks in pieces:
        draws = jnp.exp(jax.random.uniform(jax.random.fold_in(own, axis_at), (blocks,), jnp.float32, low / len(pieces), top_value / len(pieces)))
        gain = gain * jnp.repeat(draws, extent[axis_at] // blocks).reshape([-1 if axis == axis_at else 1 for axis in range(len(extent))])
    return gain


def bell_draw(stream_key, extent, deviation, most, cuts=(), kind=jnp.bfloat16):
    loudness = shard_levels(stream_key, extent, cuts, -0.22, 0.18) if cuts else 1.0
    array = jax.random.normal(stream_key, extent, jnp.float32) * deviation * loudness
    return jnp.minimum(jnp.maximum(array, -most), most).astype(kind)


def setup_inputs(seed: int = 0) -> dict:
    keys = jax.random.split(jax.random.key(seed), 11)
    return {
        "state": bell_draw(keys[0], (COLS, FEAT, LEV), 1.0, 6.0, ((0, 32),)),
        "cosine_zenith": jnp.clip(0.25 + 0.75 * jax.random.uniform(keys[1], (COLS,), jnp.float32) ** shard_levels(keys[1], (COLS,), ((0, 32),), -0.2, 0.2), 0.25, 1.0).astype(jnp.bfloat16),
        "sunlit": draw_sunlit(jax.random.fold_in(keys[10], 71), 0),
        "kcoef": bell_draw(keys[3], (FEAT, G), FEAT ** -0.5, 1.0),
        "scatter_coef": bell_draw(keys[4], (FEAT, G), FEAT ** -0.5, 1.0),
        "gpoint_weight": jnp.clip(jnp.exp(jax.random.uniform(keys[5], (G,), jnp.float32, math.log(0.3), math.log(3.0))), 0.3, 3.0),
        "sea_temp": bell_draw(keys[6], (OCELLS,), 1.0, 6.0, ((0, 32),), jnp.float32),
        "intersection_col": place_ends(jax.random.randint(keys[7], (OCELLS, NOV), 0, N_CPL * COL_DEV), jax.random.fold_in(keys[7], 1), 0, (N_CPL * COL_DEV) - 1).astype(jnp.int32),
        "intersection_weight": place_ends(jax.random.randint(keys[8], (OCELLS, NOV), 1, 9), jax.random.fold_in(keys[8], 1), 1, 8).astype(jnp.int32),
        "nearest_ocean": place_ends(jax.random.randint(keys[9], (COLS,), 0, N_CPL * OCN_DEV), jax.random.fold_in(keys[9], 1), 0, (N_CPL * OCN_DEV) - 1).astype(jnp.int32),
    }


depth_scale = 0.01
relax_keep = 0.75
forcing = 4.0
block_cols = 32


def column_optics(state_blk, cosine_blk, kcoef, scatter_coef, weights):
    levels = state_blk.shape[2]
    gpoints = kcoef.shape[1]
    state32 = state_blk.astype(jnp.float32)
    proj_abs = jnp.einsum("cfl,fg->clg", state32, kcoef.astype(jnp.float32), precision=lax.Precision.HIGHEST)
    proj_sca = jnp.einsum("cfl,fg->clg", state32, scatter_coef.astype(jnp.float32), precision=lax.Precision.HIGHEST)
    soft_abs = jax.nn.softplus(proj_abs)
    soft_sca = jax.nn.softplus(proj_sca)
    extinction = (depth_scale * (soft_abs + soft_sca)).astype(jnp.bfloat16)
    share = soft_abs / (soft_abs + soft_sca)
    row_index = lax.broadcasted_iota(jnp.int32, (levels, levels), 0)
    col_index = lax.broadcasted_iota(jnp.int32, (levels, levels), 1)
    upper = (row_index < col_index).astype(jnp.float32)
    ext32 = extinction.astype(jnp.float32)
    above = jnp.einsum("cmg,ml->clg", ext32, upper, precision=lax.Precision.HIGHEST)
    cosine = cosine_blk.astype(jnp.float32)
    lit_col = cosine > 0.0
    safe_cos = jnp.where(lit_col, cosine, jnp.float32(1.0))
    inverse = 1.0 / safe_cos
    downward = safe_cos[:, None, None] * jnp.exp(-above * inverse[:, None, None])
    absorbed = share * downward * (1.0 - jnp.exp(-ext32 * inverse[:, None, None]))
    heating = jnp.sum(absorbed * weights, axis=-1) * (levels / gpoints)
    bottom = safe_cos[:, None] * jnp.exp(-(above[:, -1, :] + ext32[:, -1, :]) * inverse[:, None])
    surface = jnp.sum(bottom * weights, axis=-1) / gpoints
    heating = jnp.where(lit_col[:, None], heating, jnp.float32(0.0))
    surface = jnp.where(lit_col, surface, jnp.float32(0.0))
    return heating, surface


def reference(state, cosine_zenith, sunlit, kcoef, scatter_coef, gpoint_weight, sea_temp, intersection_col, intersection_weight, nearest_ocean):
    cosine_eff = cosine_zenith * sunlit.astype(cosine_zenith.dtype)
    total = state.shape[0]
    block_count = total // block_cols
    state_blocks = state.reshape(block_count, block_cols, state.shape[1], state.shape[2])
    cosine_blocks = cosine_eff.reshape(block_count, block_cols)

    def one_block(pair):
        return column_optics(pair[0], pair[1], kcoef, scatter_coef, gpoint_weight)

    heating, surface = lax.map(one_block, (state_blocks, cosine_blocks))
    heating = heating.reshape(total, state.shape[2])
    surface = surface.reshape(total)
    cells = sea_temp.shape[0]
    cell_base = (jnp.arange(cells, dtype=jnp.int32) // (OCN_DEV * N_CPL)) * (N_CPL * COL_DEV)
    picked = surface[cell_base[:, None] + intersection_col]
    weight_f = intersection_weight.astype(jnp.float32)
    ocean_flux = jnp.sum(weight_f * picked, axis=-1) / jnp.sum(weight_f, axis=-1)
    sea_next = relax_keep * sea_temp + forcing * ocean_flux
    column_base = (jnp.arange(total, dtype=jnp.int32) // (COL_DEV * N_CPL)) * (N_CPL * OCN_DEV)
    column_sea = sea_next[column_base + nearest_ocean]
    return heating, sea_next, column_sea
```

```python
import functools

import jax
import jax.numpy as jnp
from jax import lax
from jax.experimental import pallas as pl
from jax.experimental.pallas import tpu as pltpu
from jax.sharding import PartitionSpec as P

depth_scale = 0.01
relax_keep = 0.75
forcing = 4.0
group_cols = 4
chunk_g = 64
log2e = 1.4426950408889634


def soft_plus(x):
    y = jnp.exp(jnp.minimum(x, 87.0))
    lifted = jnp.where(y < 1e-4, y - 0.5 * y * y, jnp.log(1.0 + y))
    return jnp.maximum(x, lifted)


def radiation_kernel(
    sunlit_ref, cosine_ref, state_ref, kabs_ref, ksca_ref, upper_ref, wide_ref, weight_ref,
    heat_ref, surf_ref, order_ref, ext_ref, part_ref,
):
    columns, levels = heat_ref.shape
    gpoints = kabs_ref.shape[0]
    heat_ref[...] = jnp.zeros_like(heat_ref)
    part_ref[...] = jnp.zeros_like(part_ref)

    def note(step, found):
        for inner in range(8):
            col = step * 8 + inner
            order_ref[found] = col
            found = found + sunlit_ref[col]
        return found

    count = lax.fori_loop(0, columns // 8, note, jnp.int32(0))
    row_id = lax.broadcasted_iota(jnp.int32, (8, 2 * levels), 0)
    lane_id = lax.broadcasted_iota(jnp.int32, (8, 2 * levels), 1)
    select = ((lane_id // levels) == row_id).astype(jnp.bfloat16)
    row8 = lax.broadcasted_iota(jnp.int32, (8, gpoints), 0)
    lane1 = lax.broadcasted_iota(jnp.int32, (1, 2 * levels), 1)

    def group(step, carry):
        for pair in range(group_cols // 2):
            base = step * group_cols + 2 * pair
            first, second = order_ref[base], order_ref[base + 1]
            u_first, u_second = cosine_ref[first], cosine_ref[second]
            u_lane = jnp.where(lane1 < levels, u_first, u_second)
            rate = -1.0 / u_lane
            both = jnp.concatenate([state_ref[first], state_ref[second]], axis=1)
            total = jnp.zeros((8, 2 * levels), jnp.float32)
            for low in range(0, gpoints, chunk_g):
                rows = slice(low, low + chunk_g)
                soft_abs = soft_plus(
                    jnp.dot(kabs_ref[rows], both, preferred_element_type=jnp.float32)
                )
                soft_sca = soft_plus(
                    jnp.dot(ksca_ref[rows], both, preferred_element_type=jnp.float32)
                )
                soft = soft_abs + soft_sca
                ext = (depth_scale * soft).astype(jnp.bfloat16)
                ext_ref[pair, rows] = ext
                above = jnp.dot(ext, upper_ref[...], preferred_element_type=jnp.float32)
                reach = jnp.exp(above * rate - jnp.log(soft))
                lost = 1.0 - jnp.exp(ext.astype(jnp.float32) * rate)
                term = soft_abs * reach * (lost * wide_ref[rows])
                total = total + jnp.sum(term.reshape(chunk_g // 8, 8, 2 * levels), axis=0)
            row = jnp.sum(total, axis=0, keepdims=True) * (u_lane * (levels / gpoints))
            heat_ref[pl.ds(first, 1), :] = row[:, :levels]
            heat_ref[pl.ds(second, 1), :] = row[:, levels:]
            depth = lax.dot_general(
                select, ext_ref[pair], (((1,), (1,)), ((), ())),
                preferred_element_type=jnp.float32,
            )
            u_row = jnp.where(row8 == 0, u_first, u_second)
            bottom = u_row * jnp.exp(-depth / u_row) * (weight_ref[...] / gpoints)
            half = bottom[:, : gpoints // 2] + bottom[:, gpoints // 2 :]
            part_ref[pl.ds(first, 1), :] = half[0:1]
            part_ref[pl.ds(second, 1), :] = half[1:2]
        return carry

    lax.fori_loop(0, count // group_cols, group, jnp.int32(0))
    surf_ref[...] = jnp.sum(part_ref[...].reshape(columns // 128, 128, 128), axis=-1)


def radiation(sunlit, cosine, state, kcoef, scatter_coef, weights):
    columns, feats, levels = state.shape
    gpoints = kcoef.shape[1]
    row_index = lax.broadcasted_iota(jnp.int32, (2 * levels, 2 * levels), 0)
    col_index = lax.broadcasted_iota(jnp.int32, (2 * levels, 2 * levels), 1)
    same = (row_index // levels) == (col_index // levels)
    upper = (same & (row_index < col_index)).astype(jnp.bfloat16)
    wide = jnp.broadcast_to(weights[:, None], (gpoints, 2 * levels))
    vmem = pl.BlockSpec(memory_space=pltpu.VMEM)
    smem = pl.BlockSpec(memory_space=pltpu.SMEM)
    return pl.pallas_call(
        radiation_kernel,
        out_shape=(
            jax.ShapeDtypeStruct((columns, levels), jnp.float32),
            jax.ShapeDtypeStruct((columns // 128, 128), jnp.float32),
        ),
        in_specs=[smem, smem, vmem, vmem, vmem, vmem, vmem, vmem],
        out_specs=(vmem, vmem),
        scratch_shapes=[
            pltpu.SMEM((columns + 8,), jnp.int32),
            pltpu.VMEM((group_cols // 2, gpoints, 2 * levels), jnp.bfloat16),
            pltpu.VMEM((columns, 128), jnp.float32),
        ],
        compiler_params=pltpu.CompilerParams(vmem_limit_bytes=40 * 1024 * 1024),
        name="radiation",
    )(sunlit, cosine, state, kcoef.T, scatter_coef.T, upper, wide, weights[None, :])


def pick(table, index):
    low = index % 128
    high = index // 128
    found = jnp.zeros(index.shape, jnp.float32)
    for row in range(table.shape[0]):
        line = jnp.broadcast_to(table[row : row + 1], index.shape)
        found = jnp.where(high == row, jnp.take_along_axis(line, low, axis=1), found)
    return found


def ocean_kernel(flux_ref, icol_ref, iweight_ref, sea_ref, next_ref):
    picked = pick(flux_ref[...], icol_ref[...])
    weight = iweight_ref[...].astype(jnp.float32)
    product = weight * picked
    rows = sea_ref.shape[0]
    overlaps = weight.shape[0] // rows
    top = product[:rows]
    bottom = weight[:rows]
    for k in range(1, overlaps):
        top = top + product[k * rows : (k + 1) * rows]
        bottom = bottom + weight[k * rows : (k + 1) * rows]
    next_ref[...] = relax_keep * sea_ref[...] + forcing * (top / bottom)


def column_kernel(sea_ref, near_ref, out_ref):
    out_ref[...] = pick(sea_ref[...], near_ref[...])


def local(
    state, cosine_zenith, sunlit, kcoef, scatter_coef, gpoint_weight, sea_temp,
    intersection_col, intersection_weight, nearest_ocean,
):
    cosine = cosine_zenith.astype(jnp.float32)
    cells = sea_temp.shape[0]
    heating, surface = radiation(sunlit, cosine, state, kcoef, scatter_coef, gpoint_weight)
    icol = intersection_col.T.reshape(-1, 128)
    iweight = intersection_weight.T.reshape(-1, 128)
    section_flux = lax.all_gather(surface, "cpl", axis=0, tiled=True)
    sea_next = pl.pallas_call(
        ocean_kernel,
        out_shape=jax.ShapeDtypeStruct((cells // 128, 128), jnp.float32),
        name="ocean",
    )(section_flux, icol, iweight, sea_temp.reshape(-1, 128))
    section_sea = lax.all_gather(sea_next, "cpl", axis=0, tiled=True)
    column_sea = pl.pallas_call(
        column_kernel,
        out_shape=jax.ShapeDtypeStruct((nearest_ocean.shape[0] // 128, 128), jnp.float32),
        name="column",
    )(section_sea, nearest_ocean.reshape(-1, 128))
    return (heating, sea_next.reshape(-1), column_sea.reshape(-1))


def solution(mesh):
    both = ("atm", "cpl")
    return jax.shard_map(
        local,
        mesh=mesh,
        in_specs=(
            P(both, None, None), P(both), P(both), P(), P(), P(), P(both),
            P(both, None), P(both, None), P(both),
        ),
        out_specs=(P(both, None), P(both), P(both)),
        check_vma=False,
    )
```

```python
import functools

import jax
import jax.numpy as jnp
from jax import lax
from jax.experimental import pallas as pl
from jax.experimental.pallas import tpu as pltpu
from jax.sharding import PartitionSpec as P

depth_scale = 0.01
relax_keep = 0.75
forcing = 4.0
group_cols = 8
moved_cols = 144
chunk_g = 64
log2e = 1.4426950408889634
ln2 = 0.6931471805599453


def soft_plus2(t):
    y = jnp.exp2(jnp.minimum(t, 126.0))
    lifted = jnp.where(y < 1e-4, y * (log2e - (0.5 * log2e) * y), lax.log2(1.0 + y))
    return jnp.maximum(t, lifted)


def pack_kernel(sunlit_ref, cosine_ref, state_ref, packed_ref, sent_ref, order_ref, meta_ref):
    columns = state_ref.shape[0]
    moved = packed_ref.shape[0]

    def note(step, found):
        for inner in range(8):
            col = step * 8 + inner
            order_ref[found] = col
            found = found + sunlit_ref[col]
        return found

    count = lax.fori_loop(0, columns // 8, note, jnp.int32(0))
    excess = jnp.clip(count - columns // 2, 0, moved)
    base = count - excess
    meta_ref[0] = base
    meta_ref[1] = excess

    def copy(step, carry):
        for inner in range(8):
            slot = step * 8 + inner
            col = order_ref[base + slot]
            packed_ref[slot] = state_ref[col]
            sent_ref[slot] = cosine_ref[col]
        return carry

    def blank(slot, carry):
        sent_ref[slot] = jnp.float32(0.0)
        return carry

    lax.fori_loop(0, excess // 8, copy, jnp.int32(0))
    lax.fori_loop(excess, moved, blank, jnp.int32(0))


def merge_kernel(order_ref, meta_ref, surf_in_ref, heat_in_ref, part_in_ref, back_ref, heat_ref, surf_ref, part_ref):
    heat_ref[...] = heat_in_ref[...]
    part_ref[...] = part_in_ref[...]
    base, excess = meta_ref[0], meta_ref[1]
    lane = lax.broadcasted_iota(jnp.int32, (1, 128), 1)

    def put(step, carry):
        for inner in range(8):
            slot = step * 8 + inner
            col = order_ref[base + slot]
            heat_ref[pl.ds(col, 1), :] = back_ref[pl.ds(slot, 1), :]
            part_ref[pl.ds(col, 1), :] = jnp.where(lane == 0, surf_in_ref[slot], 0.0)
        return carry

    lax.fori_loop(0, excess // 8, put, jnp.int32(0))
    columns = heat_ref.shape[0]
    surf_ref[...] = jnp.sum(part_ref[...].reshape(columns // 128, 128, 128), axis=-1)


def radiation_kernel(
    order_ref, count_ref, cosine_ref, state_ref, kabs_ref, ksca_ref, upper_ref, wide_ref, weight_ref,
    heat_ref, part_ref, ext_ref,
):
    columns, levels = heat_ref.shape
    gpoints = kabs_ref.shape[0]
    heat_ref[...] = jnp.zeros_like(heat_ref)
    part_ref[...] = jnp.zeros_like(part_ref)
    count = count_ref[0]
    row_id = lax.broadcasted_iota(jnp.int32, (8, 2 * levels), 0)
    lane_id = lax.broadcasted_iota(jnp.int32, (8, 2 * levels), 1)
    select = ((lane_id // levels) == row_id).astype(jnp.bfloat16)
    row8 = lax.broadcasted_iota(jnp.int32, (8, gpoints), 0)
    start = lax.broadcasted_iota(jnp.int32, (chunk_g, 2 * levels), 1) % levels == 0
    lane1 = lax.broadcasted_iota(jnp.int32, (1, 2 * levels), 1)

    def group(step, carry):
        for pair in range(group_cols // 2):
            base = step * group_cols + 2 * pair
            first, second = order_ref[base], order_ref[base + 1]
            u_first, u_second = cosine_ref[first], cosine_ref[second]
            u_lane = jnp.where(lane1 < levels, u_first, u_second)
            rate = -log2e / u_lane
            both = jnp.concatenate([state_ref[first], state_ref[second]], axis=1)
            both = jnp.concatenate([both, both, both], axis=0)
            total = jnp.zeros((8, 2 * levels), jnp.float32)
            for low in range(0, gpoints, chunk_g):
                rows = slice(low, low + chunk_g)
                soft_abs = soft_plus2(
                    jnp.dot(kabs_ref[rows], both, preferred_element_type=jnp.float32)
                )
                soft_sca = soft_plus2(
                    jnp.dot(ksca_ref[rows], both, preferred_element_type=jnp.float32)
                )
                soft = soft_abs + soft_sca
                ext = ((depth_scale * ln2) * soft).astype(jnp.bfloat16)
                ext_ref[pair, rows] = ext
                through = jnp.dot(ext, upper_ref[...], preferred_element_type=jnp.float32)
                leave = jnp.exp2(through * rate)
                enter = jnp.where(start, 1.0, pltpu.roll(leave, 1, 1))
                share = soft_abs * pl.reciprocal(soft, approx=False)
                term = share * (enter - leave) * wide_ref[rows]
                total = total + jnp.sum(term.reshape(chunk_g // 8, 8, 2 * levels), axis=0)
            row = jnp.sum(total, axis=0, keepdims=True) * (u_lane * (levels / gpoints))
            heat_ref[pl.ds(first, 1), :] = row[:, :levels]
            heat_ref[pl.ds(second, 1), :] = row[:, levels:]
            depth = lax.dot_general(
                select, ext_ref[pair], (((1,), (1,)), ((), ())),
                preferred_element_type=jnp.float32,
            )
            u_row = jnp.where(row8 == 0, u_first, u_second)
            bottom = u_row * jnp.exp(-depth / u_row) * (weight_ref[...] / gpoints)
            half = bottom[:, : gpoints // 2] + bottom[:, gpoints // 2 :]
            part_ref[pl.ds(first, 1), :] = half[0:1]
            part_ref[pl.ds(second, 1), :] = half[1:2]
        return carry

    lax.fori_loop(0, count // group_cols, group, jnp.int32(0))


def split_terms(coef):
    scaled = coef.T.astype(jnp.float32) * log2e
    high = lax.reduce_precision(scaled, 8, 7)
    middle = lax.reduce_precision(scaled - high, 8, 7)
    low = scaled - high - middle
    return jnp.concatenate([high, middle, low], axis=1).astype(jnp.bfloat16)


def tables(kcoef, scatter_coef, weights, levels):
    row_index = lax.broadcasted_iota(jnp.int32, (2 * levels, 2 * levels), 0)
    col_index = lax.broadcasted_iota(jnp.int32, (2 * levels, 2 * levels), 1)
    same = (row_index // levels) == (col_index // levels)
    upper = (same & (row_index <= col_index)).astype(jnp.bfloat16)
    wide = jnp.broadcast_to(weights[:, None], (weights.shape[0], 2 * levels))
    return split_terms(kcoef), split_terms(scatter_coef), upper, wide, weights[None, :]


vmem = pl.BlockSpec(memory_space=pltpu.VMEM)
smem = pl.BlockSpec(memory_space=pltpu.SMEM)


def pack(sunlit, cosine, state, moved):
    columns, feats, levels = state.shape
    return pl.pallas_call(
        pack_kernel,
        out_shape=(
            jax.ShapeDtypeStruct((moved, feats, levels), state.dtype),
            jax.ShapeDtypeStruct((moved,), jnp.float32),
            jax.ShapeDtypeStruct((columns + 8,), jnp.int32),
            jax.ShapeDtypeStruct((8,), jnp.int32),
        ),
        in_specs=[smem, smem, vmem],
        out_specs=(vmem, smem, smem, smem),
        compiler_params=pltpu.CompilerParams(vmem_limit_bytes=16 * 1024 * 1024),
        name="pack",
    )(sunlit, cosine, state)


def radiation(order, count, cosine, state, constants):
    columns, feats, levels = state.shape
    gpoints = constants[0].shape[0]
    return pl.pallas_call(
        radiation_kernel,
        out_shape=(
            jax.ShapeDtypeStruct((columns, levels), jnp.float32),
            jax.ShapeDtypeStruct((columns, 128), jnp.float32),
        ),
        in_specs=[smem, smem, smem, vmem, vmem, vmem, vmem, vmem, vmem],
        out_specs=(vmem, vmem),
        scratch_shapes=[
            pltpu.VMEM((group_cols // 2, gpoints, 2 * levels), jnp.bfloat16),
        ],
        compiler_params=pltpu.CompilerParams(vmem_limit_bytes=24 * 1024 * 1024),
        cost_estimate=pl.CostEstimate(
            flops=columns * levels * gpoints * 1000,
            bytes_accessed=columns * feats * levels * 2,
            transcendentals=columns * levels * gpoints * 6,
        ),
        name="radiation",
    )(order, count, cosine, state, *constants)


def merge(order, meta, surf_back, heat, part, back):
    columns, levels = heat.shape
    return pl.pallas_call(
        merge_kernel,
        out_shape=(
            jax.ShapeDtypeStruct((columns, levels), jnp.float32),
            jax.ShapeDtypeStruct((columns // 128, 128), jnp.float32),
        ),
        in_specs=[smem, smem, smem, vmem, vmem, vmem],
        out_specs=(vmem, vmem),
        scratch_shapes=[pltpu.VMEM((columns, 128), jnp.float32)],
        name="merge",
    )(order, meta, surf_back, heat, part, back)


def balanced(sunlit, cosine, state, kcoef, scatter_coef, weights):
    levels = state.shape[2]
    atm_count = lax.axis_size("atm")
    swap = [(i, (i + atm_count // 2) % atm_count) for i in range(atm_count)]
    constants = tables(kcoef, scatter_coef, weights, levels)
    packed, sent, order, meta = pack(sunlit, cosine, state, moved_cols)
    guest = lax.ppermute(packed, "atm", swap)
    guest_cosine = lax.ppermute(sent, "atm", swap)
    heat, part = radiation(order, meta, cosine, state, constants)
    guest_count = jnp.sum((guest_cosine > 0).astype(jnp.int32)).reshape(1)
    guest_heat, guest_part = radiation(
        jnp.arange(moved_cols, dtype=jnp.int32), guest_count, guest_cosine, guest, constants
    )
    guest_surf = jnp.sum(guest_part, axis=-1)
    back = lax.ppermute(guest_heat, "atm", swap)
    surf_back = lax.ppermute(guest_surf, "atm", swap)
    return merge(order, meta, surf_back, heat, part, back)


def pick(table, index):
    low = index % 128
    high = index // 128
    found = jnp.zeros(index.shape, jnp.float32)
    for row in range(table.shape[0]):
        line = jnp.broadcast_to(table[row : row + 1], index.shape)
        found = jnp.where(high == row, jnp.take_along_axis(line, low, axis=1), found)
    return found


def ocean_kernel(flux_ref, icol_ref, iweight_ref, sea_ref, next_ref):
    picked = pick(flux_ref[...], icol_ref[...])
    weight = iweight_ref[...].astype(jnp.float32)
    product = weight * picked
    rows = sea_ref.shape[0]
    overlaps = weight.shape[0] // rows
    top = product[:rows]
    bottom = weight[:rows]
    for k in range(1, overlaps):
        top = top + product[k * rows : (k + 1) * rows]
        bottom = bottom + weight[k * rows : (k + 1) * rows]
    next_ref[...] = relax_keep * sea_ref[...] + forcing * (top / bottom)


def column_kernel(sea_ref, near_ref, out_ref):
    out_ref[...] = pick(sea_ref[...], near_ref[...])


def local(
    state, cosine_zenith, sunlit, kcoef, scatter_coef, gpoint_weight, sea_temp,
    intersection_col, intersection_weight, nearest_ocean,
):
    cosine = cosine_zenith.astype(jnp.float32)
    cells = sea_temp.shape[0]
    heating, surface = balanced(sunlit, cosine, state, kcoef, scatter_coef, gpoint_weight)
    icol = intersection_col.T.reshape(-1, 128)
    iweight = intersection_weight.T.reshape(-1, 128)
    section_flux = lax.all_gather(surface, "cpl", axis=0, tiled=True)
    sea_next = pl.pallas_call(
        ocean_kernel,
        out_shape=jax.ShapeDtypeStruct((cells // 128, 128), jnp.float32),
        name="ocean",
    )(section_flux, icol, iweight, sea_temp.reshape(-1, 128))
    section_sea = lax.all_gather(sea_next, "cpl", axis=0, tiled=True)
    column_sea = pl.pallas_call(
        column_kernel,
        out_shape=jax.ShapeDtypeStruct((nearest_ocean.shape[0] // 128, 128), jnp.float32),
        name="column",
    )(section_sea, nearest_ocean.reshape(-1, 128))
    return (heating, sea_next.reshape(-1), column_sea.reshape(-1))


def solution(mesh):
    both = ("atm", "cpl")
    return jax.shard_map(
        local,
        mesh=mesh,
        in_specs=(
            P(both, None, None), P(both), P(both), P(), P(), P(), P(both),
            P(both, None), P(both, None), P(both),
        ),
        out_specs=(P(both, None), P(both), P(both)),
        check_vma=False,
    )
```

```python
import functools

import jax
import jax.numpy as jnp
from jax import lax
from jax.experimental import pallas as pl
from jax.experimental.pallas import tpu as pltpu
from jax.sharding import PartitionSpec as P

depth_scale = 0.01
relax_keep = 0.75
forcing = 4.0
group_cols = 8
moved_cols = 144
chunk_g = 64
log2e = 1.4426950408889634
ln2 = 0.6931471805599453


def soft_plus2(t):
    y = jnp.exp2(jnp.minimum(t, 126.0))
    lifted = jnp.where(y < 1e-4, y * (log2e - (0.5 * log2e) * y), lax.log2(1.0 + y))
    return jnp.maximum(t, lifted)


def pack_kernel(sunlit_ref, cosine_ref, state_ref, packed_ref, sent_ref, order_ref, meta_ref):
    columns = state_ref.shape[0]
    moved = packed_ref.shape[0]

    def note(step, found):
        for inner in range(8):
            col = step * 8 + inner
            order_ref[found] = col
            found = found + sunlit_ref[col]
        return found

    count = lax.fori_loop(0, columns // 8, note, jnp.int32(0))
    excess = jnp.clip(count - columns // 2, 0, moved)
    base = count - excess
    meta_ref[0] = base
    meta_ref[1] = excess

    def copy(step, carry):
        for inner in range(8):
            slot = step * 8 + inner
            col = order_ref[base + slot]
            packed_ref[slot] = state_ref[col]
            sent_ref[slot] = cosine_ref[col]
        return carry

    def blank(slot, carry):
        sent_ref[slot] = jnp.float32(0.0)
        return carry

    lax.fori_loop(0, excess // 8, copy, jnp.int32(0))
    lax.fori_loop(excess, moved, blank, jnp.int32(0))


def merge_kernel(order_ref, meta_ref, surf_in_ref, heat_in_ref, part_in_ref, back_ref, heat_ref, surf_ref, part_ref):
    heat_ref[...] = heat_in_ref[...]
    part_ref[...] = part_in_ref[...]
    base, excess = meta_ref[0], meta_ref[1]
    lane = lax.broadcasted_iota(jnp.int32, (1, 128), 1)

    def put(step, carry):
        for inner in range(8):
            slot = step * 8 + inner
            col = order_ref[base + slot]
            heat_ref[pl.ds(col, 1), :] = back_ref[pl.ds(slot, 1), :]
            part_ref[pl.ds(col, 1), :] = jnp.where(lane == 0, surf_in_ref[slot], 0.0)
        return carry

    lax.fori_loop(0, excess // 8, put, jnp.int32(0))
    columns = heat_ref.shape[0]
    surf_ref[...] = jnp.sum(part_ref[...].reshape(columns // 128, 128, 128), axis=-1)


def radiation_kernel(
    order_ref, count_ref, cosine_ref, state_ref, kabs_ref, ksca_ref, upper_ref, wide_ref, weight_ref,
    heat_ref, part_ref, ext_ref,
):
    columns, levels = heat_ref.shape
    gpoints = kabs_ref.shape[0]
    heat_ref[...] = jnp.zeros_like(heat_ref)
    part_ref[...] = jnp.zeros_like(part_ref)
    count = count_ref[0]
    row_id = lax.broadcasted_iota(jnp.int32, (8, 2 * levels), 0)
    lane_id = lax.broadcasted_iota(jnp.int32, (8, 2 * levels), 1)
    select = ((lane_id // levels) == row_id).astype(jnp.bfloat16)
    row8 = lax.broadcasted_iota(jnp.int32, (8, gpoints), 0)
    start = lax.broadcasted_iota(jnp.int32, (chunk_g, 2 * levels), 1) % levels == 0
    lane1 = lax.broadcasted_iota(jnp.int32, (1, 2 * levels), 1)

    def group(step, carry):
        for pair in range(group_cols // 2):
            base = step * group_cols + 2 * pair
            first, second = order_ref[base], order_ref[base + 1]
            u_first, u_second = cosine_ref[first], cosine_ref[second]
            u_lane = jnp.where(lane1 < levels, u_first, u_second)
            rate = -log2e / u_lane
            both = jnp.concatenate([state_ref[first], state_ref[second]], axis=1)
            both = jnp.concatenate([both, both, both], axis=0)
            total = jnp.zeros((8, 2 * levels), jnp.float32)
            for low in range(0, gpoints, chunk_g):
                rows = slice(low, low + chunk_g)
                soft_abs = soft_plus2(
                    jnp.dot(kabs_ref[rows], both, preferred_element_type=jnp.float32)
                )
                soft_sca = soft_plus2(
                    jnp.dot(ksca_ref[rows], both, preferred_element_type=jnp.float32)
                )
                soft = soft_abs + soft_sca
                ext = ((depth_scale * ln2) * soft).astype(jnp.bfloat16)
                ext_ref[pair, rows] = ext
                through = jnp.dot(ext, upper_ref[...], preferred_element_type=jnp.float32)
                leave = jnp.exp2(through * rate)
                enter = jnp.where(start, 1.0, pltpu.roll(leave, 1, 1))
                share = soft_abs * pl.reciprocal(soft, approx=False)
                term = share * (enter - leave) * wide_ref[rows]
                total = total + jnp.sum(term.reshape(chunk_g // 8, 8, 2 * levels), axis=0)
            row = jnp.sum(total, axis=0, keepdims=True) * (u_lane * (levels / gpoints))
            heat_ref[pl.ds(first, 1), :] = row[:, :levels]
            heat_ref[pl.ds(second, 1), :] = row[:, levels:]
            depth = lax.dot_general(
                select, ext_ref[pair], (((1,), (1,)), ((), ())),
                preferred_element_type=jnp.float32,
            )
            u_row = jnp.where(row8 == 0, u_first, u_second)
            bottom = u_row * jnp.exp(-depth / u_row) * (weight_ref[...] / gpoints)
            half = bottom[:, : gpoints // 2] + bottom[:, gpoints // 2 :]
            part_ref[pl.ds(first, 1), :] = half[0:1]
            part_ref[pl.ds(second, 1), :] = half[1:2]
        return carry

    lax.fori_loop(0, count // group_cols, group, jnp.int32(0))


def split_terms(coef):
    scaled = coef.T.astype(jnp.float32) * log2e
    high = lax.reduce_precision(scaled, 8, 7)
    middle = lax.reduce_precision(scaled - high, 8, 7)
    low = scaled - high - middle
    return jnp.concatenate([high, middle, low], axis=1).astype(jnp.bfloat16)


def tables(kcoef, scatter_coef, weights, levels):
    row_index = lax.broadcasted_iota(jnp.int32, (2 * levels, 2 * levels), 0)
    col_index = lax.broadcasted_iota(jnp.int32, (2 * levels, 2 * levels), 1)
    same = (row_index // levels) == (col_index // levels)
    upper = (same & (row_index <= col_index)).astype(jnp.bfloat16)
    wide = jnp.broadcast_to(weights[:, None], (weights.shape[0], 2 * levels))
    return split_terms(kcoef), split_terms(scatter_coef), upper, wide, weights[None, :]


vmem = pl.BlockSpec(memory_space=pltpu.VMEM)
smem = pl.BlockSpec(memory_space=pltpu.SMEM)


def pack(sunlit, cosine, state, moved):
    columns, feats, levels = state.shape
    return pl.pallas_call(
        pack_kernel,
        out_shape=(
            jax.ShapeDtypeStruct((moved, feats, levels), state.dtype),
            jax.ShapeDtypeStruct((moved,), jnp.float32),
            jax.ShapeDtypeStruct((columns + 8,), jnp.int32),
            jax.ShapeDtypeStruct((8,), jnp.int32),
        ),
        in_specs=[smem, smem, vmem],
        out_specs=(vmem, smem, smem, smem),
        compiler_params=pltpu.CompilerParams(vmem_limit_bytes=16 * 1024 * 1024),
        name="pack",
    )(sunlit, cosine, state)


def radiation(order, count, cosine, state, constants):
    columns, feats, levels = state.shape
    gpoints = constants[0].shape[0]
    return pl.pallas_call(
        radiation_kernel,
        out_shape=(
            jax.ShapeDtypeStruct((columns, levels), jnp.float32),
            jax.ShapeDtypeStruct((columns, 128), jnp.float32),
        ),
        in_specs=[smem, smem, smem, vmem, vmem, vmem, vmem, vmem, vmem],
        out_specs=(vmem, vmem),
        scratch_shapes=[
            pltpu.VMEM((group_cols // 2, gpoints, 2 * levels), jnp.bfloat16),
        ],
        compiler_params=pltpu.CompilerParams(vmem_limit_bytes=24 * 1024 * 1024),
        cost_estimate=pl.CostEstimate(
            flops=columns * levels * gpoints * 1000,
            bytes_accessed=columns * feats * levels * 2,
            transcendentals=columns * levels * gpoints * 6,
        ),
        name="radiation",
    )(order, count, cosine, state, *constants)


def merge(order, meta, surf_back, heat, part, back):
    columns, levels = heat.shape
    return pl.pallas_call(
        merge_kernel,
        out_shape=(
            jax.ShapeDtypeStruct((columns, levels), jnp.float32),
            jax.ShapeDtypeStruct((columns // 128, 128), jnp.float32),
        ),
        in_specs=[smem, smem, smem, vmem, vmem, vmem],
        out_specs=(vmem, vmem),
        scratch_shapes=[pltpu.VMEM((columns, 128), jnp.float32)],
        name="merge",
    )(order, meta, surf_back, heat, part, back)


def balanced(sunlit, cosine, state, kcoef, scatter_coef, weights):
    levels = state.shape[2]
    atm_count = lax.axis_size("atm")
    swap = [(i, (i + atm_count // 2) % atm_count) for i in range(atm_count)]
    constants = tables(kcoef, scatter_coef, weights, levels)
    packed, sent, order, meta = pack(sunlit, cosine, state, moved_cols)
    guest = lax.ppermute(packed, "atm", swap)
    guest_cosine = lax.ppermute(sent, "atm", swap)
    heat, part = radiation(order, meta, cosine, state, constants)
    guest, guest_cosine, heat, part = lax.optimization_barrier((guest, guest_cosine, heat, part))
    guest_count = jnp.sum((guest_cosine > 0).astype(jnp.int32)).reshape(1)
    guest_heat, guest_part = radiation(
        jnp.arange(moved_cols, dtype=jnp.int32), guest_count, guest_cosine, guest, constants
    )
    guest_surf = jnp.sum(guest_part, axis=-1)
    back = lax.ppermute(guest_heat, "atm", swap)
    surf_back = lax.ppermute(guest_surf, "atm", swap)
    return merge(order, meta, surf_back, heat, part, back)


def pick(table, index):
    low = index % 128
    high = index // 128
    found = jnp.zeros(index.shape, jnp.float32)
    for row in range(table.shape[0]):
        line = jnp.broadcast_to(table[row : row + 1], index.shape)
        found = jnp.where(high == row, jnp.take_along_axis(line, low, axis=1), found)
    return found


def ocean_kernel(flux_ref, icol_ref, iweight_ref, sea_ref, next_ref):
    picked = pick(flux_ref[...], icol_ref[...])
    weight = iweight_ref[...].astype(jnp.float32)
    product = weight * picked
    rows = sea_ref.shape[0]
    overlaps = weight.shape[0] // rows
    top = product[:rows]
    bottom = weight[:rows]
    for k in range(1, overlaps):
        top = top + product[k * rows : (k + 1) * rows]
        bottom = bottom + weight[k * rows : (k + 1) * rows]
    next_ref[...] = relax_keep * sea_ref[...] + forcing * (top / bottom)


def column_kernel(sea_ref, near_ref, out_ref):
    out_ref[...] = pick(sea_ref[...], near_ref[...])


def local(
    state, cosine_zenith, sunlit, kcoef, scatter_coef, gpoint_weight, sea_temp,
    intersection_col, intersection_weight, nearest_ocean,
):
    cosine = cosine_zenith.astype(jnp.float32)
    cells = sea_temp.shape[0]
    heating, surface = balanced(sunlit, cosine, state, kcoef, scatter_coef, gpoint_weight)
    icol = intersection_col.T.reshape(-1, 128)
    iweight = intersection_weight.T.reshape(-1, 128)
    section_flux = lax.all_gather(surface, "cpl", axis=0, tiled=True)
    sea_next = pl.pallas_call(
        ocean_kernel,
        out_shape=jax.ShapeDtypeStruct((cells // 128, 128), jnp.float32),
        name="ocean",
    )(section_flux, icol, iweight, sea_temp.reshape(-1, 128))
    section_sea = lax.all_gather(sea_next, "cpl", axis=0, tiled=True)
    column_sea = pl.pallas_call(
        column_kernel,
        out_shape=jax.ShapeDtypeStruct((nearest_ocean.shape[0] // 128, 128), jnp.float32),
        name="column",
    )(section_sea, nearest_ocean.reshape(-1, 128))
    return (heating, sea_next.reshape(-1), column_sea.reshape(-1))


def solution(mesh):
    both = ("atm", "cpl")
    return jax.shard_map(
        local,
        mesh=mesh,
        in_specs=(
            P(both, None, None), P(both), P(both), P(), P(), P(), P(both),
            P(both, None), P(both, None), P(both),
        ),
        out_specs=(P(both, None), P(both), P(both)),
        check_vma=False,
    )
```

```python
import functools

import jax
import jax.numpy as jnp
from jax import lax
from jax.experimental import pallas as pl
from jax.experimental.pallas import tpu as pltpu
from jax.sharding import PartitionSpec as P

depth_scale = 0.01
relax_keep = 0.75
forcing = 4.0
group_cols = 8
moved_cols = 152
chunk_g = 64
log2e = 1.4426950408889634
ln2 = 0.6931471805599453


def soft_plus2(t):
    y = jnp.exp2(jnp.minimum(t, 126.0))
    lifted = jnp.where(y < 1e-4, y * (log2e - (0.5 * log2e) * y), lax.log2(1.0 + y))
    return jnp.maximum(t, lifted)


def pack_kernel(sunlit_ref, cosine_ref, state_ref, packed_ref, sent_ref, order_ref, meta_ref):
    columns = state_ref.shape[0]
    moved = packed_ref.shape[0]

    def note(step, found):
        for inner in range(8):
            col = step * 8 + inner
            order_ref[found] = col
            found = found + sunlit_ref[col]
        return found

    count = lax.fori_loop(0, columns // 8, note, jnp.int32(0))
    excess = jnp.clip(count - columns // 2, 0, moved)
    base = count - excess
    meta_ref[0] = base
    meta_ref[1] = excess

    def copy(step, carry):
        for inner in range(8):
            slot = step * 8 + inner
            col = order_ref[base + slot]
            packed_ref[slot] = state_ref[col]
            sent_ref[slot] = cosine_ref[col]
        return carry

    def blank(slot, carry):
        sent_ref[slot] = jnp.float32(0.0)
        return carry

    lax.fori_loop(0, excess // 8, copy, jnp.int32(0))
    lax.fori_loop(excess, moved, blank, jnp.int32(0))


def merge_kernel(order_ref, meta_ref, surf_in_ref, heat_in_ref, part_in_ref, back_ref, heat_ref, surf_ref, part_ref):
    heat_ref[...] = heat_in_ref[...]
    part_ref[...] = part_in_ref[...]
    base, excess = meta_ref[0], meta_ref[1]
    lane = lax.broadcasted_iota(jnp.int32, (1, 128), 1)

    def put(step, carry):
        for inner in range(8):
            slot = step * 8 + inner
            col = order_ref[base + slot]
            heat_ref[pl.ds(col, 1), :] = back_ref[pl.ds(slot, 1), :]
            part_ref[pl.ds(col, 1), :] = jnp.where(lane == 0, surf_in_ref[slot], 0.0)
        return carry

    lax.fori_loop(0, excess // 8, put, jnp.int32(0))
    columns = heat_ref.shape[0]
    surf_ref[...] = jnp.sum(part_ref[...].reshape(columns // 128, 128, 128), axis=-1)


def radiation_kernel(
    order_ref, count_ref, cosine_ref, state_ref, kboth_ref, upper_ref, wide_ref, weight_ref,
    heat_ref, part_ref, ext_ref,
):
    columns, levels = heat_ref.shape
    gpoints = wide_ref.shape[0]
    heat_ref[...] = jnp.zeros_like(heat_ref)
    part_ref[...] = jnp.zeros_like(part_ref)
    count = count_ref[0]
    row_id = lax.broadcasted_iota(jnp.int32, (8, 2 * levels), 0)
    lane_id = lax.broadcasted_iota(jnp.int32, (8, 2 * levels), 1)
    select = ((lane_id // levels) == row_id).astype(jnp.bfloat16)
    row8 = lax.broadcasted_iota(jnp.int32, (8, gpoints), 0)
    start = lax.broadcasted_iota(jnp.int32, (chunk_g, 2 * levels), 1) % levels == 0
    lane1 = lax.broadcasted_iota(jnp.int32, (1, 2 * levels), 1)

    def group(step, carry):
        for pair in range(group_cols // 2):
            base = step * group_cols + 2 * pair
            first, second = order_ref[base], order_ref[base + 1]
            u_first, u_second = cosine_ref[first], cosine_ref[second]
            u_lane = jnp.where(lane1 < levels, u_first, u_second)
            rate = -log2e / u_lane
            both = jnp.concatenate([state_ref[first], state_ref[second]], axis=1)
            both = jnp.concatenate([both, both, both], axis=0)
            total = jnp.zeros((8, 2 * levels), jnp.float32)
            for low in range(0, gpoints, chunk_g):
                rows = slice(low, low + chunk_g)
                proj = jnp.dot(
                    kboth_ref[2 * low : 2 * low + 2 * chunk_g], both,
                    preferred_element_type=jnp.float32,
                )
                soft_abs = soft_plus2(proj[:chunk_g])
                soft_sca = soft_plus2(proj[chunk_g:])
                soft = soft_abs + soft_sca
                ext = ((depth_scale * ln2) * soft).astype(jnp.bfloat16)
                ext_ref[pair, rows] = ext
                through = jnp.dot(ext, upper_ref[...], preferred_element_type=jnp.float32)
                leave = jnp.exp2(through * rate)
                enter = jnp.where(start, 1.0, pltpu.roll(leave, 1, 1))
                share = soft_abs * pl.reciprocal(soft, approx=False)
                term = share * (enter - leave) * wide_ref[rows]
                total = total + jnp.sum(term.reshape(chunk_g // 8, 8, 2 * levels), axis=0)
            row = jnp.sum(total, axis=0, keepdims=True) * (u_lane * (levels / gpoints))
            heat_ref[pl.ds(first, 1), :] = row[:, :levels]
            heat_ref[pl.ds(second, 1), :] = row[:, levels:]
            depth = lax.dot_general(
                select, ext_ref[pair], (((1,), (1,)), ((), ())),
                preferred_element_type=jnp.float32,
            )
            u_row = jnp.where(row8 == 0, u_first, u_second)
            bottom = u_row * jnp.exp(-depth / u_row) * (weight_ref[...] / gpoints)
            half = bottom[:, : gpoints // 2] + bottom[:, gpoints // 2 :]
            part_ref[pl.ds(first, 1), :] = half[0:1]
            part_ref[pl.ds(second, 1), :] = half[1:2]
        return carry

    lax.fori_loop(0, count // group_cols, group, jnp.int32(0))


def split_terms(coef):
    scaled = coef.T.astype(jnp.float32) * log2e
    high = lax.reduce_precision(scaled, 8, 7)
    middle = lax.reduce_precision(scaled - high, 8, 7)
    low = scaled - high - middle
    return jnp.concatenate([high, middle, low], axis=1).astype(jnp.bfloat16)


def tables(kcoef, scatter_coef, weights, levels):
    row_index = lax.broadcasted_iota(jnp.int32, (2 * levels, 2 * levels), 0)
    col_index = lax.broadcasted_iota(jnp.int32, (2 * levels, 2 * levels), 1)
    same = (row_index // levels) == (col_index // levels)
    upper = (same & (row_index <= col_index)).astype(jnp.bfloat16)
    wide = jnp.broadcast_to(weights[:, None], (weights.shape[0], 2 * levels))
    pieces = jnp.stack([split_terms(kcoef), split_terms(scatter_coef)])
    pieces = pieces.reshape(2, -1, chunk_g, pieces.shape[2]).transpose(1, 0, 2, 3)
    return pieces.reshape(-1, pieces.shape[3]), upper, wide, weights[None, :]


vmem = pl.BlockSpec(memory_space=pltpu.VMEM)
smem = pl.BlockSpec(memory_space=pltpu.SMEM)


def pack(sunlit, cosine, state, moved):
    columns, feats, levels = state.shape
    return pl.pallas_call(
        pack_kernel,
        out_shape=(
            jax.ShapeDtypeStruct((moved, feats, levels), state.dtype),
            jax.ShapeDtypeStruct((moved,), jnp.float32),
            jax.ShapeDtypeStruct((columns + 8,), jnp.int32),
            jax.ShapeDtypeStruct((8,), jnp.int32),
        ),
        in_specs=[smem, smem, vmem],
        out_specs=(vmem, smem, smem, smem),
        compiler_params=pltpu.CompilerParams(vmem_limit_bytes=16 * 1024 * 1024),
        name="pack",
    )(sunlit, cosine, state)


def radiation(order, count, cosine, state, constants):
    columns, feats, levels = state.shape
    gpoints = constants[2].shape[0]
    return pl.pallas_call(
        radiation_kernel,
        out_shape=(
            jax.ShapeDtypeStruct((columns, levels), jnp.float32),
            jax.ShapeDtypeStruct((columns, 128), jnp.float32),
        ),
        in_specs=[smem, smem, smem, vmem, vmem, vmem, vmem, vmem],
        out_specs=(vmem, vmem),
        scratch_shapes=[
            pltpu.VMEM((group_cols // 2, gpoints, 2 * levels), jnp.bfloat16),
        ],
        compiler_params=pltpu.CompilerParams(vmem_limit_bytes=24 * 1024 * 1024),
        cost_estimate=pl.CostEstimate(
            flops=columns * levels * gpoints * 1000,
            bytes_accessed=columns * feats * levels * 2,
            transcendentals=columns * levels * gpoints * 6,
        ),
        name="radiation",
    )(order, count, cosine, state, *constants)


def merge(order, meta, surf_back, heat, part, back):
    columns, levels = heat.shape
    return pl.pallas_call(
        merge_kernel,
        out_shape=(
            jax.ShapeDtypeStruct((columns, levels), jnp.float32),
            jax.ShapeDtypeStruct((columns // 128, 128), jnp.float32),
        ),
        in_specs=[smem, smem, smem, vmem, vmem, vmem],
        out_specs=(vmem, vmem),
        scratch_shapes=[pltpu.VMEM((columns, 128), jnp.float32)],
        name="merge",
    )(order, meta, surf_back, heat, part, back)


def balanced(sunlit, cosine, state, kcoef, scatter_coef, weights):
    levels = state.shape[2]
    atm_count = lax.axis_size("atm")
    swap = [(i, (i + atm_count // 2) % atm_count) for i in range(atm_count)]
    constants = tables(kcoef, scatter_coef, weights, levels)
    packed, sent, order, meta = pack(sunlit, cosine, state, moved_cols)
    guest = lax.ppermute(packed, "atm", swap)
    guest_cosine = lax.ppermute(sent, "atm", swap)
    heat, part = radiation(order, meta, cosine, state, constants)
    guest, guest_cosine, heat, part = lax.optimization_barrier((guest, guest_cosine, heat, part))
    guest_count = jnp.sum((guest_cosine > 0).astype(jnp.int32)).reshape(1)
    guest_heat, guest_part = radiation(
        jnp.arange(moved_cols, dtype=jnp.int32), guest_count, guest_cosine, guest, constants
    )
    guest_surf = jnp.sum(guest_part, axis=-1)
    back = lax.ppermute(guest_heat, "atm", swap)
    surf_back = lax.ppermute(guest_surf, "atm", swap)
    return merge(order, meta, surf_back, heat, part, back)


def pick(table, index):
    low = index % 128
    high = index // 128
    found = jnp.zeros(index.shape, jnp.float32)
    for row in range(table.shape[0]):
        line = jnp.broadcast_to(table[row : row + 1], index.shape)
        found = jnp.where(high == row, jnp.take_along_axis(line, low, axis=1), found)
    return found


def ocean_kernel(flux_ref, icol_ref, iweight_ref, sea_ref, next_ref):
    picked = pick(flux_ref[...], icol_ref[...])
    weight = iweight_ref[...].astype(jnp.float32)
    product = weight * picked
    rows = sea_ref.shape[0]
    overlaps = weight.shape[0] // rows
    top = product[:rows]
    bottom = weight[:rows]
    for k in range(1, overlaps):
        top = top + product[k * rows : (k + 1) * rows]
        bottom = bottom + weight[k * rows : (k + 1) * rows]
    next_ref[...] = relax_keep * sea_ref[...] + forcing * (top / bottom)


def column_kernel(sea_ref, near_ref, out_ref):
    out_ref[...] = pick(sea_ref[...], near_ref[...])


def local(
    state, cosine_zenith, sunlit, kcoef, scatter_coef, gpoint_weight, sea_temp,
    intersection_col, intersection_weight, nearest_ocean,
):
    cosine = cosine_zenith.astype(jnp.float32)
    cells = sea_temp.shape[0]
    heating, surface = balanced(sunlit, cosine, state, kcoef, scatter_coef, gpoint_weight)
    icol = intersection_col.T.reshape(-1, 128)
    iweight = intersection_weight.T.reshape(-1, 128)
    section_flux = lax.all_gather(surface, "cpl", axis=0, tiled=True)
    sea_next = pl.pallas_call(
        ocean_kernel,
        out_shape=jax.ShapeDtypeStruct((cells // 128, 128), jnp.float32),
        name="ocean",
    )(section_flux, icol, iweight, sea_temp.reshape(-1, 128))
    section_sea = lax.all_gather(sea_next, "cpl", axis=0, tiled=True)
    column_sea = pl.pallas_call(
        column_kernel,
        out_shape=jax.ShapeDtypeStruct((nearest_ocean.shape[0] // 128, 128), jnp.float32),
        name="column",
    )(section_sea, nearest_ocean.reshape(-1, 128))
    return (heating, sea_next.reshape(-1), column_sea.reshape(-1))


def solution(mesh):
    both = ("atm", "cpl")
    return jax.shard_map(
        local,
        mesh=mesh,
        in_specs=(
            P(both, None, None), P(both), P(both), P(), P(), P(), P(both),
            P(both, None), P(both, None), P(both),
        ),
        out_specs=(P(both, None), P(both), P(both)),
        check_vma=False,
    )
```
